32 devices in a mesh: var: 8 (over y, x, core), smp: 4 (over z).
Axes of the slice: x: 2, y: 2, z: 4, core: 2. Of those that a mesh axis runs over, the one named last changes fastest.
Arguments:
- dosage: bfloat16 [4096, 4096], P('smp', 'var'), may hold values from -6 to 6
- trait_class: int32 [4096], P('smp'), may hold values from 0 to 15
- class_effect: float32 [16], replicated, may hold values from -4 to 4
Outputs:
- interaction: float32 [4096, 1536], P(('var', 'smp'))
The draws below stay inside these ranges and needn't reach their ends.
All inputs are finite; a program needn't handle non-finite values.
Results may differ from the reference program's by a relative error of at most 0.0029.
Values may be sent and summed in bfloat16 or wider, within the bound.
A program may use at most 64 MiB of HBM per device.

```python
import jax
import jax.numpy as jnp
from jax import lax

VAR_DEV = 512
CLASSES = 16
SAMPLES = 4096
VARIANTS = 4096
N_VAR = 8


def set_ends(drawn, key, least, high):
    longest = drawn.shape.index(max(drawn.shape))
    spots = []
    for shift in (0, 1):
        where = [jax.random.randint(jax.random.fold_in(key, axis), (), 0, length) for axis, length in enumerate(drawn.shape)]
        where[longest] = (where[longest] + shift) % drawn.shape[longest]
        spots.append(tuple(where))
    return drawn.at[spots[0]].set(least).at[spots[1]].set(high)


def steps_of(key, shape, cuts, least, largest):
    def one(dim, blocks):
        draws = jax.random.uniform(jax.random.fold_in(jax.random.fold_in(key, 6), dim), (blocks,), jnp.float32, least / len(cuts), largest / len(cuts))
        return jnp.repeat(jnp.exp(draws), shape[dim] // blocks).reshape((-1,) + (1,) * (len(shape) - dim - 1))

    factor_of = one(*cuts[0])
    for cut in cuts[1:]:
        factor_of = factor_of * one(*cut)
    return factor_of


def bell_draw(rng, dims, scale, most, cuts=(), kind=jnp.bfloat16):
    gain = steps_of(rng, dims, cuts, -0.22, 0.18) if cuts else 1.0
    drawn = jax.random.normal(rng, dims, jnp.float32) * scale * gain
    return jnp.minimum(jnp.maximum(drawn, -most), most).astype(kind)


def setup_inputs(seed: int = 0) -> dict:
    seeds = jax.random.split(jax.random.key(seed), 4)
    return {
        "dosage": bell_draw(seeds[0], (SAMPLES, VARIANTS), 1.0, 6.0, ((0, 4), (1, 8))),
        "trait_class": set_ends(jax.random.randint(seeds[1], (SAMPLES,), 0, CLASSES), jax.random.fold_in(seeds[1], 1), 0, CLASSES - 1).astype(jnp.int32),
        "class_effect": bell_draw(seeds[2], (CLASSES,), 1.0, 4.0, (), jnp.float32),
    }


def reference(dosage, trait_class, class_effect):
    centred = class_effect - jnp.mean(class_effect)
    picks = trait_class[:, None] == jnp.arange(CLASSES, dtype=jnp.int32)[None, :]
    trait = lax.optimization_barrier(jnp.sum(jnp.where(picks, centred[None, :], jnp.float32(0.0)), axis=1))

    def one_block(block):

        def take(index):
            start = (jnp.mod(index, N_VAR) * VAR_DEV).astype(jnp.int32)
            return lax.dynamic_slice_in_dim(dosage, start, VAR_DEV, 1)
        own = take(block)
        right = jnp.concatenate([take(block - 1), own, take(block + 1)], axis=1)
        own_values = own.astype(jnp.float32)
        weighted = (trait[:, None] * own_values).astype(jnp.bfloat16)
        squared = (own_values * own_values).astype(jnp.bfloat16)
        right_values = right.astype(jnp.float32)
        right_sq = (right_values * right_values).astype(jnp.bfloat16)
        cross = jnp.dot(weighted.T, right, preferred_element_type=jnp.float32)
        fourth = jnp.dot(squared.T, right_sq, preferred_element_type=jnp.float32)
        return cross / jnp.sqrt(fourth + 1e-05)
    blocks = lax.map(one_block, jnp.arange(N_VAR, dtype=jnp.int32))
    return blocks.reshape(VARIANTS, 3 * VAR_DEV)
```

```python
import functools

import jax
import jax.numpy as jnp
from jax import lax
from jax.experimental import pallas as pl
from jax.experimental.pallas import tpu as pltpu
from jax.sharding import PartitionSpec as P

MESH = pl.DeviceIdType.MESH
F32, BF16 = jnp.float32, jnp.bfloat16


def kernel(
    nv, n, d_ref, class_ref, effect_ref, out_ref,
    after, wt, qt, sq, part, wire, relay, fwd, summed, direct, turned, before,
    d_send, d_recv, relay_send, relay_recv, fwd_send, sum_recv, dir_send, dir_recv, t_send, t_recv,
):
    depth, width = d_ref.shape
    rows = width // n
    pairs = n // 2
    v, s = lax.axis_index("var"), lax.axis_index("smp")
    nxt, prv = lax.rem(v + 1, nv), lax.rem(v + nv - 1, nv)
    pair, odd = s // 2, lax.rem(s, 2)
    partner = s + 1 - 2 * odd

    barrier = pltpu.get_barrier_semaphore()
    for step in range(1, n):
        pl.semaphore_signal(barrier, inc=1, device_id=(v, lax.rem(s + step, n)), device_id_type=MESH)
    for step in range(n):
        for near in (nxt, prv):
            pl.semaphore_signal(barrier, inc=1, device_id=(near, lax.rem(s + step, n)), device_id_type=MESH)
    pl.semaphore_wait(barrier, 3 * n - 1)

    shift = pltpu.make_async_remote_copy(
        src_ref=d_ref, dst_ref=after, send_sem=d_send, recv_sem=d_recv,
        device_id=(prv, s), device_id_type=MESH,
    )
    shift.start()

    classes = effect_ref.shape[0]
    mean = effect_ref[0]
    for c in range(1, classes):
        mean = mean + effect_ref[c]
    mean = mean / classes
    picked = class_ref[...]
    trait = jnp.zeros(picked.shape, F32)
    for c in range(classes):
        trait = jnp.where(picked == c, effect_ref[c] - mean, trait)
    for at in range(0, width, 128):
        cols = d_ref[:, at:at + 128].astype(F32).T
        wt[at:at + 128, :] = (cols * trait).astype(BF16)
        qt[at:at + 128, :] = (cols * cols).astype(BF16)

    def squares(ref):
        values = ref[...].astype(F32)
        sq[...] = (values * values).astype(BF16)

    def at_rows(index, count=1):
        return pl.ds(pl.multiple_of(index * rows, rows), count * rows)

    def relay_copy(u, k):
        other = lax.rem(pair + k, pairs)
        return pltpu.make_async_remote_copy(
            src_ref=wire.at[u, at_rows(2 * other, 2)], dst_ref=relay.at[u, k - 1],
            send_sem=relay_send.at[u, k - 1], recv_sem=relay_recv.at[u, k - 1],
            device_id=(v, partner), device_id_type=MESH,
        )

    def fwd_copy(u, k, j):
        other = lax.rem(pair + k, pairs)
        return pltpu.make_async_remote_copy(
            src_ref=fwd.at[u, k - 1, j], dst_ref=summed.at[u, pairs - k - 1],
            send_sem=fwd_send.at[u, k - 1, j], recv_sem=sum_recv.at[u, pairs - k - 1],
            device_id=(v, 2 * other + j), device_id_type=MESH,
        )

    def dir_copy(u):
        return pltpu.make_async_remote_copy(
            src_ref=wire.at[u, at_rows(partner)], dst_ref=direct.at[u],
            send_sem=dir_send.at[u], recv_sem=dir_recv.at[u],
            device_id=(v, partner), device_id_type=MESH,
        )

    def outer(k):
        higher = lax.rem(pair + k, pairs) > pair
        return jnp.logical_or(
            jnp.logical_and(higher, odd == 0), jnp.logical_and(jnp.logical_not(higher), odd == 1)
        )

    def product(u, left, right):
        got = jnp.dot(left[...], right[...], preferred_element_type=F32)
        part[u] = got
        wire[u] = got.astype(BF16)

    def send_relays(u):
        for k in range(1, pairs):
            @pl.when(outer(k))
            def _():
                relay_copy(u, k).start()

    def send_sums(u):
        for k in range(1, pairs):
            @pl.when(jnp.logical_not(outer(k)))
            def _():
                relay_copy(u, k).wait_recv()
                other = lax.rem(pair + k, pairs)
                for j in range(2):
                    own = part[u, at_rows(2 * other + j), :]
                    got = relay[u, k - 1, j * rows:(j + 1) * rows, :].astype(F32)
                    fwd[u, k - 1, j] = (own + got).astype(BF16)
                    fwd_copy(u, k, j).start()

    def total(u):
        got = part[u, at_rows(s), :]
        dir_copy(u).wait_recv()
        got = got + direct[u].astype(F32)
        for k in range(1, pairs):
            fwd_copy(u, k, 0).wait_recv()
            got = got + summed[u, pairs - k - 1].astype(F32)
        return got

    product(0, wt, d_ref)
    send_relays(0)
    squares(d_ref)
    product(1, qt, sq)
    send_relays(1)
    dir_copy(0).start()
    dir_copy(1).start()
    shift.wait_recv()
    product(2, wt, after)
    send_relays(2)
    squares(after)
    product(3, qt, sq)
    send_relays(3)
    dir_copy(2).start()
    dir_copy(3).start()
    for u in range(4):
        send_sums(u)

    cross = total(2)
    fourth = total(3)
    stat = cross / jnp.sqrt(fourth + 1e-05)
    out_ref[:, 2 * width:] = stat
    turned[...] = stat.T.astype(BF16)

    def turn_copy(t):
        return pltpu.make_async_remote_copy(
            src_ref=turned.at[t * rows:(t + 1) * rows], dst_ref=before.at[s],
            send_sem=t_send.at[t], recv_sem=t_recv.at[s],
            device_id=(nxt, t), device_id_type=MESH,
        )

    def turn_wait(t):
        return pltpu.make_async_remote_copy(
            src_ref=turned.at[t * rows:(t + 1) * rows], dst_ref=before.at[t],
            send_sem=t_send.at[t], recv_sem=t_recv.at[t],
            device_id=(nxt, t), device_id_type=MESH,
        )

    for t in range(n):
        turn_copy(t).start()
    cross = total(0)
    fourth = total(1)
    out_ref[:, width:2 * width] = cross / jnp.sqrt(fourth + 1e-05)
    for t in range(n):
        turn_wait(t).wait_recv()
        out_ref[:, t * rows:(t + 1) * rows] = before[t].astype(F32)

    shift.wait_send()
    for u in range(4):
        dir_copy(u).wait_send()
        for k in range(1, pairs):
            @pl.when(outer(k))
            def _():
                relay_copy(u, k).wait_send()

            @pl.when(jnp.logical_not(outer(k)))
            def _():
                for j in range(2):
                    fwd_copy(u, k, j).wait_send()
    for t in range(n):
        turn_wait(t).wait_send()


def solution(mesh):
    nv, n = mesh.shape["var"], mesh.shape["smp"]

    def shards(dosage, trait_class, class_effect):
        depth, width = dosage.shape
        rows, far = width // n, max(n // 2 - 1, 1)
        dma = pltpu.SemaphoreType.DMA
        return pl.pallas_call(
            functools.partial(kernel, nv, n),
            out_shape=jax.ShapeDtypeStruct((rows, 3 * width), F32),
            in_specs=[
                pl.BlockSpec(memory_space=pltpu.VMEM),
                pl.BlockSpec(memory_space=pltpu.VMEM),
                pl.BlockSpec(memory_space=pltpu.SMEM),
            ],
            out_specs=pl.BlockSpec(memory_space=pltpu.VMEM),
            scratch_shapes=[
                pltpu.VMEM((depth, width), BF16),
                pltpu.VMEM((width, depth), BF16),
                pltpu.VMEM((width, depth), BF16),
                pltpu.VMEM((depth, width), BF16),
                pltpu.VMEM((4, width, width), F32),
                pltpu.VMEM((4, width, width), BF16),
                pltpu.VMEM((4, far, 2 * rows, width), BF16),
                pltpu.VMEM((4, far, 2, rows, width), BF16),
                pltpu.VMEM((4, far, rows, width), BF16),
                pltpu.VMEM((4, rows, width), BF16),
                pltpu.VMEM((width, rows), BF16),
                pltpu.VMEM((n, rows, rows), BF16),
                dma, dma,
                dma((4, far)), dma((4, far)),
                dma((4, far, 2)), dma((4, far)),
                dma((4,)), dma((4,)),
                dma((n,)), dma((n,)),
            ],
            compiler_params=pltpu.CompilerParams(
                collective_id=0, has_side_effects=True, vmem_limit_bytes=60 * 1024 * 1024
            ),
        )(dosage, trait_class.reshape(1, depth), class_effect)

    in_specs = (P("smp", "var"), P("smp"), P())
    out_specs = P(("var", "smp"), None)
    return jax.shard_map(shards, mesh=mesh, in_specs=in_specs, out_specs=out_specs, check_vma=False)
```

```python
import functools

import jax
import jax.numpy as jnp
from jax import lax
from jax.experimental import pallas as pl
from jax.experimental.pallas import tpu as pltpu
from jax.sharding import PartitionSpec as P

MESH = pl.DeviceIdType.MESH
F32, BF16 = jnp.float32, jnp.bfloat16


def kernel(
    nv, n, d_ref, class_ref, effect_ref, out_ref,
    after, wt, qt, sq, part, wire, relay, fwd, summed, direct, turned, before,
    d_send, d_recv, relay_send, relay_recv, fwd_send, sum_recv, dir_send, dir_recv, t_send, t_recv,
):
    depth, width = d_ref.shape
    rows = width // n
    pairs = n // 2
    v, s = lax.axis_index("var"), lax.axis_index("smp")
    nxt, prv = lax.rem(v + 1, nv), lax.rem(v + nv - 1, nv)
    pair, odd = s // 2, lax.rem(s, 2)
    partner = s + 1 - 2 * odd

    barrier = pltpu.get_barrier_semaphore()
    for step in range(1, n):
        pl.semaphore_signal(barrier, inc=1, device_id=(v, lax.rem(s + step, n)), device_id_type=MESH)
    for step in range(n):
        for near in (nxt, prv):
            pl.semaphore_signal(barrier, inc=1, device_id=(near, lax.rem(s + step, n)), device_id_type=MESH)
    pl.semaphore_wait(barrier, 3 * n - 1)

    half = width // 2

    def cols(h):
        return slice(h * half, (h + 1) * half)

    def shift(h):
        return pltpu.make_async_remote_copy(
            src_ref=d_ref.at[:, cols(h)], dst_ref=after.at[:, cols(h)],
            send_sem=d_send.at[h], recv_sem=d_recv.at[h],
            device_id=(prv, s), device_id_type=MESH,
        )

    for h in range(2):
        shift(h).start()

    classes = effect_ref.shape[0]
    mean = effect_ref[0]
    for c in range(1, classes):
        mean = mean + effect_ref[c]
    mean = mean / classes
    picked = class_ref[...]
    trait = jnp.zeros(picked.shape, F32)
    for c in range(classes):
        trait = jnp.where(picked == c, effect_ref[c] - mean, trait)
    for at in range(0, width, 128):
        values = d_ref[:, at:at + 128].astype(F32).T
        wt[at:at + 128, :] = (values * trait).astype(BF16)
        qt[at:at + 128, :] = (values * values).astype(BF16)

    def at_rows(index, count=1):
        return pl.ds(pl.multiple_of(index * rows, rows), count * rows)

    def relay_copy(u, k):
        other = lax.rem(pair + k, pairs)
        return pltpu.make_async_remote_copy(
            src_ref=wire.at[u, at_rows(2 * other, 2)], dst_ref=relay.at[u, k - 1],
            send_sem=relay_send.at[u, k - 1], recv_sem=relay_recv.at[u, k - 1],
            device_id=(v, partner), device_id_type=MESH,
        )

    def fwd_copy(u, k, j):
        other = lax.rem(pair + k, pairs)
        return pltpu.make_async_remote_copy(
            src_ref=fwd.at[u, k - 1, j], dst_ref=summed.at[u, pairs - k - 1],
            send_sem=fwd_send.at[u, k - 1, j], recv_sem=sum_recv.at[u, pairs - k - 1],
            device_id=(v, 2 * other + j), device_id_type=MESH,
        )

    def dir_copy(u):
        return pltpu.make_async_remote_copy(
            src_ref=wire.at[u, at_rows(partner)], dst_ref=direct.at[u],
            send_sem=dir_send.at[u], recv_sem=dir_recv.at[u],
            device_id=(v, partner), device_id_type=MESH,
        )

    def outer(k):
        higher = lax.rem(pair + k, pairs) > pair
        return jnp.logical_or(
            jnp.logical_and(higher, odd == 0), jnp.logical_and(jnp.logical_not(higher), odd == 1)
        )

    def products(block, h):
        right = (after if block else d_ref)[:, cols(h)]
        u = 4 * block + 2 * h
        product(u, jnp.dot(wt[...], right, preferred_element_type=F32))
        values = right.astype(F32)
        sq[...] = (values * values).astype(BF16)
        product(u + 1, jnp.dot(qt[...], sq[...], preferred_element_type=F32))

    def product(u, got):
        part[u] = got
        wire[u] = got.astype(BF16)
        send_relays(u)

    def send_relays(u):
        for k in range(1, pairs):
            @pl.when(outer(k))
            def _():
                relay_copy(u, k).start()

    def send_sums(u):
        for k in range(1, pairs):
            @pl.when(jnp.logical_not(outer(k)))
            def _():
                relay_copy(u, k).wait_recv()
                other = lax.rem(pair + k, pairs)
                for j in range(2):
                    own = part[u, at_rows(2 * other + j), :]
                    got = relay[u, k - 1, j * rows:(j + 1) * rows, :].astype(F32)
                    fwd[u, k - 1, j] = (own + got).astype(BF16)
                    fwd_copy(u, k, j).start()

    def total(u):
        got = part[u, at_rows(s), :]
        dir_copy(u).wait_recv()
        got = got + direct[u].astype(F32)
        for k in range(1, pairs):
            fwd_copy(u, k, 0).wait_recv()
            got = got + summed[u, pairs - k - 1].astype(F32)
        return got

    for h in range(2):
        products(0, h)
    shift(0).wait_recv()
    products(1, 0)
    send_sums(0)
    send_sums(1)
    shift(1).wait_recv()
    products(1, 1)
    for u in range(4, 8):
        dir_copy(u).start()
    for u in range(4):
        dir_copy(u).start()
    for u in range(2, 8):
        send_sums(u)

    def turn_copy(t):
        return pltpu.make_async_remote_copy(
            src_ref=turned.at[t * rows:(t + 1) * rows], dst_ref=before.at[s],
            send_sem=t_send.at[t], recv_sem=t_recv.at[s],
            device_id=(nxt, t), device_id_type=MESH,
        )

    def turn_wait(t):
        return pltpu.make_async_remote_copy(
            src_ref=turned.at[t * rows:(t + 1) * rows], dst_ref=before.at[t],
            send_sem=t_send.at[t], recv_sem=t_recv.at[t],
            device_id=(nxt, t), device_id_type=MESH,
        )

    for h in range(2):
        stat = total(4 + 2 * h) / jnp.sqrt(total(5 + 2 * h) + 1e-05)
        out_ref[:, 2 * width + h * half:2 * width + (h + 1) * half] = stat
        turned[cols(h), :] = stat.T.astype(BF16)
        for t in range(h * pairs, (h + 1) * pairs):
            turn_copy(t).start()
    for h in range(2):
        stat = total(2 * h) / jnp.sqrt(total(2 * h + 1) + 1e-05)
        out_ref[:, width + h * half:width + (h + 1) * half] = stat
    for t in range(n):
        turn_wait(t).wait_recv()
        out_ref[:, t * rows:(t + 1) * rows] = before[t].astype(F32)

    for h in range(2):
        shift(h).wait_send()
    for u in range(8):
        dir_copy(u).wait_send()
        for k in range(1, pairs):
            @pl.when(outer(k))
            def _():
                relay_copy(u, k).wait_send()

            @pl.when(jnp.logical_not(outer(k)))
            def _():
                for j in range(2):
                    fwd_copy(u, k, j).wait_send()
    for t in range(n):
        turn_wait(t).wait_send()


def solution(mesh):
    nv, n = mesh.shape["var"], mesh.shape["smp"]

    def shards(dosage, trait_class, class_effect):
        depth, width = dosage.shape
        rows, half, far = width // n, width // 2, max(n // 2 - 1, 1)
        dma = pltpu.SemaphoreType.DMA
        return pl.pallas_call(
            functools.partial(kernel, nv, n),
            out_shape=jax.ShapeDtypeStruct((rows, 3 * width), F32),
            in_specs=[
                pl.BlockSpec(memory_space=pltpu.VMEM),
                pl.BlockSpec(memory_space=pltpu.VMEM),
                pl.BlockSpec(memory_space=pltpu.SMEM),
            ],
            out_specs=pl.BlockSpec(memory_space=pltpu.VMEM),
            scratch_shapes=[
                pltpu.VMEM((depth, width), BF16),
                pltpu.VMEM((width, depth), BF16),
                pltpu.VMEM((width, depth), BF16),
                pltpu.VMEM((depth, half), BF16),
                pltpu.VMEM((8, width, half), F32),
                pltpu.VMEM((8, width, half), BF16),
                pltpu.VMEM((8, far, 2 * rows, half), BF16),
                pltpu.VMEM((8, far, 2, rows, half), BF16),
                pltpu.VMEM((8, far, rows, half), BF16),
                pltpu.VMEM((8, rows, half), BF16),
                pltpu.VMEM((width, rows), BF16),
                pltpu.VMEM((n, rows, rows), BF16),
                dma((2,)), dma((2,)),
                dma((8, far)), dma((8, far)),
                dma((8, far, 2)), dma((8, far)),
                dma((8,)), dma((8,)),
                dma((n,)), dma((n,)),
            ],
            compiler_params=pltpu.CompilerParams(
                collective_id=0, has_side_effects=True, vmem_limit_bytes=20 * 1024 * 1024
            ),
        )(dosage, trait_class.reshape(1, depth), class_effect)

    in_specs = (P("smp", "var"), P("smp"), P())
    out_specs = P(("var", "smp"), None)
    return jax.shard_map(shards, mesh=mesh, in_specs=in_specs, out_specs=out_specs, check_vma=False)
```

```python
import functools

import jax
import jax.numpy as jnp
from jax import lax
from jax.experimental import pallas as pl
from jax.experimental.pallas import tpu as pltpu
from jax.sharding import PartitionSpec as P

MESH = pl.DeviceIdType.MESH
F32, BF16 = jnp.float32, jnp.bfloat16
LANES = 128


def kernel(
    nv, n, dosage_ref, class_hbm, effect_hbm, out_ref,
    d_ref, class_ref, effect_ref, after, wt, qt, sq, turned, before, own_turned, mirrored,
    own_part, own_wire, own_relay, own_fwd, own_summed, own_direct,
    next_part, next_wire, next_relay, next_fwd, next_summed, next_direct,
    load_sem, d_send, d_recv, t_send, t_recv, m_send, m_recv,
    own_rs, own_rr, own_fs, own_sr, own_ds, own_dr,
    next_rs, next_rr, next_fs, next_sr, next_ds, next_dr,
):
    depth, width = d_ref.shape
    rows, half, pairs = width // n, width // 2, n // 2
    fold = rows % LANES == 0
    v, s = lax.axis_index("var"), lax.axis_index("smp")
    nxt, prv = lax.rem(v + 1, nv), lax.rem(v + nv - 1, nv)
    pair, odd = s // 2, lax.rem(s, 2)
    partner = s + 1 - 2 * odd

    loads = [
        pltpu.make_async_copy(dosage_ref, d_ref, load_sem.at[0]),
        pltpu.make_async_copy(class_hbm, class_ref, load_sem.at[1]),
        pltpu.make_async_copy(effect_hbm, effect_ref, load_sem.at[2]),
    ]
    for load in loads:
        load.start()
    barrier = pltpu.get_barrier_semaphore()
    for near in (nxt, prv):
        for step in range(n):
            pl.semaphore_signal(barrier, inc=1, device_id=(near, lax.rem(s + step, n)), device_id_type=MESH)
    for step in range(1, n):
        pl.semaphore_signal(barrier, inc=1, device_id=(v, lax.rem(s + step, n)), device_id_type=MESH)
    for load in loads:
        load.wait()
    pl.semaphore_wait(barrier, 3 * n - 1)

    def cols(h):
        return slice(h * half, (h + 1) * half)

    def shift(h):
        return pltpu.make_async_remote_copy(
            src_ref=d_ref.at[:, cols(h)], dst_ref=after.at[:, cols(h)],
            send_sem=d_send.at[h], recv_sem=d_recv.at[h],
            device_id=(prv, s), device_id_type=MESH,
        )

    for h in range(2):
        shift(h).start()

    classes = effect_ref.shape[0]
    mean = effect_ref[0]
    for c in range(1, classes):
        mean = mean + effect_ref[c]
    mean = mean / classes
    picked = class_ref[...]
    trait = jnp.zeros(picked.shape, F32)
    for c in range(classes):
        trait = jnp.where(picked == c, effect_ref[c] - mean, trait)
    for at in range(0, width, LANES):
        values = d_ref[:, at:at + LANES].astype(F32).T
        wt[at:at + LANES, :] = (values * trait).astype(BF16)
        qt[at:at + LANES, :] = (values * values).astype(BF16)

    def owns(a, c):
        from_a, from_c = abs_of(2 * a - (n - 1)), abs_of(2 * c - (n - 1))
        return jnp.logical_or(from_a > from_c, jnp.logical_and(from_a == from_c, a < c))

    def abs_of(x):
        return lax.max(x, -x) if isinstance(x, jax.Array) else jnp.int32(abs(x))

    def extent(t):
        if not fold:
            return slice(0, width)
        first, last = (t, n - 1 - t) if t < pairs else (n - t, t)
        return slice(first * rows, (last + 1) * rows)

    def cases(index, count, body):
        for known in range(count):
            pl.when(index == known)(functools.partial(body, known))

    def at_rows(index):
        return pl.ds(pl.multiple_of(index * rows, rows), rows)

    def outer(k):
        higher = lax.rem(pair + k, pairs) > pair
        return jnp.logical_or(
            jnp.logical_and(higher, odd == 0), jnp.logical_and(jnp.logical_not(higher), odd == 1)
        )

    class Group:
        def __init__(self, folded, part, wire, relay, fwd, summed, direct, rs, rr, fs, sr, ds, dr):
            self.folded, self.part, self.wire, self.relay = folded, part, wire, relay
            self.fwd, self.summed, self.direct = fwd, summed, direct
            self.rs, self.rr, self.fs, self.sr, self.ds, self.dr = rs, rr, fs, sr, ds, dr

        def span(self, t):
            return extent(t) if self.folded else slice(None)

        def by(self, index, count, body):
            if self.folded:
                cases(index, count, body)
            else:
                body(index)

        def relay_copy(self, u, other, j):
            t = 2 * other + j
            span = self.span(t)
            return pltpu.make_async_remote_copy(
                src_ref=self.wire.at[u, at_rows(t), span], dst_ref=self.relay.at[u, other, j, :, span],
                send_sem=self.rs.at[u, other, j], recv_sem=self.rr.at[u, other, j],
                device_id=(v, partner), device_id_type=MESH,
            )

        def fwd_copy(self, u, other, j):
            t = 2 * other + j
            span = self.span(t)
            return pltpu.make_async_remote_copy(
                src_ref=self.fwd.at[u, other, j, :, span], dst_ref=self.summed.at[u, pair, :, span],
                send_sem=self.fs.at[u, other, j], recv_sem=self.sr.at[u, pair],
                device_id=(v, t), device_id_type=MESH,
            )

        def sum_wait(self, u, source, t):
            span = self.span(t)
            here = self.summed.at[u, source, :, span]
            pltpu.make_async_remote_copy(
                src_ref=here, dst_ref=here, send_sem=self.fs.at[u, source, 0], recv_sem=self.sr.at[u, source],
                device_id=(v, partner), device_id_type=MESH,
            ).wait_recv()

        def dir_copy(self, u, t):
            span = self.span(t)
            return pltpu.make_async_remote_copy(
                src_ref=self.wire.at[u, at_rows(t), span], dst_ref=self.direct.at[u, :, span],
                send_sem=self.ds.at[u], recv_sem=self.dr.at[u],
                device_id=(v, partner), device_id_type=MESH,
            )

        def product(self, u, left, right):
            got = jnp.dot(left[...], right, preferred_element_type=F32)
            self.part[u] = got
            self.wire[u] = got.astype(BF16)
            for k in range(1, pairs):
                @pl.when(outer(k))
                def _():
                    def send(other):
                        for j in range(2):
                            self.relay_copy(u, other, j).start()

                    self.by(lax.rem(pair + k, pairs), pairs, send)

        def send_sums(self, u):
            for k in range(1, pairs):
                @pl.when(jnp.logical_not(outer(k)))
                def _():
                    def send(other):
                        for j in range(2):
                            self.relay_copy(u, other, j).wait_recv()
                            own = self.part[u, at_rows(2 * other + j), :]
                            self.fwd[u, other, j] = (own + self.relay[u, other, j].astype(F32)).astype(BF16)
                            self.fwd_copy(u, other, j).start()

                    self.by(lax.rem(pair + k, pairs), pairs, send)

        def send_direct(self, u):
            self.by(partner, n, lambda t: self.dir_copy(u, t).start())

        def total(self, u):
            def wait(t):
                self.dir_copy(u, t).wait_recv()
                for k in range(1, pairs):
                    self.sum_wait(u, lax.rem(pair + k, pairs), t)

            self.by(s, n, wait)
            got = self.part[u, at_rows(s), :] + self.direct[u].astype(F32)
            for k in range(1, pairs):
                got = got + self.summed[u, lax.rem(pair + k, pairs)].astype(F32)
            return got

        def finish(self, units):
            for u in range(units):
                self.by(partner, n, lambda t: self.dir_copy(u, t).wait_send())
                for k in range(1, pairs):
                    def relays(other):
                        for j in range(2):
                            self.relay_copy(u, other, j).wait_send()

                    def sums(other):
                        for j in range(2):
                            self.fwd_copy(u, other, j).wait_send()

                    other = lax.rem(pair + k, pairs)

                    @pl.when(outer(k))
                    def _():
                        self.by(other, pairs, relays)

                    @pl.when(jnp.logical_not(outer(k)))
                    def _():
                        self.by(other, pairs, sums)

    own = Group(
        fold, own_part, own_wire, own_relay, own_fwd, own_summed, own_direct,
        own_rs, own_rr, own_fs, own_sr, own_ds, own_dr,
    )
    follow = Group(
        False, next_part, next_wire, next_relay, next_fwd, next_summed, next_direct,
        next_rs, next_rr, next_fs, next_sr, next_ds, next_dr,
    )

    def squares(values):
        values = values.astype(F32)
        return (values * values).astype(BF16)

    own.product(0, wt, d_ref[...])
    sq[...] = squares(d_ref[...])
    own.product(1, qt, sq[...])
    for h in range(2):
        shift(h).wait_recv()
        follow.product(2 * h, wt, after[:, cols(h)])
        sq[:, cols(h)] = squares(after[:, cols(h)])
        follow.product(2 * h + 1, qt, sq[:, cols(h)])
        if h == 0:
            for u in range(2):
                own.send_sums(u)
    for u in range(4):
        follow.send_direct(u)
    for u in range(2):
        own.send_direct(u)
    for u in range(4):
        follow.send_sums(u)

    def turn_copy(t, slot):
        return pltpu.make_async_remote_copy(
            src_ref=turned.at[t * rows:(t + 1) * rows], dst_ref=before.at[slot],
            send_sem=t_send.at[t], recv_sem=t_recv.at[slot],
            device_id=(nxt, t), device_id_type=MESH,
        )

    def mirror_copy(t, slot):
        return pltpu.make_async_remote_copy(
            src_ref=own_turned.at[t * rows:(t + 1) * rows], dst_ref=mirrored.at[slot],
            send_sem=m_send.at[t], recv_sem=m_recv.at[slot],
            device_id=(v, t), device_id_type=MESH,
        )

    for h in range(2):
        stat = follow.total(2 * h) / jnp.sqrt(follow.total(2 * h + 1) + 1e-05)
        out_ref[:, 2 * width + h * half:2 * width + (h + 1) * half] = stat
        turned[cols(h), :] = stat.T.astype(BF16)
        for t in range(h * pairs, (h + 1) * pairs):
            turn_copy(t, s).start()
    stat = own.total(0) / jnp.sqrt(own.total(1) + 1e-05)
    if fold:
        own_turned[...] = stat.T.astype(BF16)
        for t in range(n):
            @pl.when(owns(s, t))
            def _():
                mirror_copy(t, s).start()
    out_ref[:, width:2 * width] = stat
    for t in range(n):
        turn_copy(t, t).wait_recv()
        out_ref[:, t * rows:(t + 1) * rows] = before[t].astype(F32)
    if fold:
        for t in range(n):
            @pl.when(owns(t, s))
            def _():
                mirror_copy(t, t).wait_recv()
                out_ref[:, width + t * rows:width + (t + 1) * rows] = mirrored[t].astype(F32)

            @pl.when(owns(s, t))
            def _():
                mirror_copy(t, t).wait_send()

    for h in range(2):
        shift(h).wait_send()
    own.finish(2)
    follow.finish(4)
    for t in range(n):
        turn_copy(t, t).wait_send()


def solution(mesh):
    nv, n = mesh.shape["var"], mesh.shape["smp"]

    def shards(dosage, trait_class, class_effect):
        depth, width = dosage.shape
        rows, half, pairs = width // n, width // 2, n // 2
        dma, vmem = pltpu.SemaphoreType.DMA, pltpu.VMEM

        def buffers(units, wide):
            return [
                vmem((units, width, wide), F32),
                vmem((units, width, wide), BF16),
                vmem((units, pairs, 2, rows, wide), BF16),
                vmem((units, pairs, 2, rows, wide), BF16),
                vmem((units, pairs, rows, wide), BF16),
                vmem((units, rows, wide), BF16),
            ]

        def semaphores(units):
            return [
                dma((units, pairs, 2)), dma((units, pairs, 2)), dma((units, pairs, 2)),
                dma((units, pairs)), dma((units,)), dma((units,)),
            ]

        return pl.pallas_call(
            functools.partial(kernel, nv, n),
            out_shape=jax.ShapeDtypeStruct((rows, 3 * width), F32),
            in_specs=[pl.BlockSpec(memory_space=pltpu.HBM)] * 3,
            out_specs=pl.BlockSpec(memory_space=vmem),
            scratch_shapes=[
                vmem((depth, width), BF16),
                vmem((1, depth), jnp.int32),
                pltpu.SMEM(class_effect.shape, F32),
                vmem((depth, width), BF16),
                vmem((width, depth), BF16),
                vmem((width, depth), BF16),
                vmem((depth, width), BF16),
                vmem((width, rows), BF16),
                vmem((n, rows, rows), BF16),
                vmem((width, rows), BF16),
                vmem((n, rows, rows), BF16),
                *buffers(2, width),
                *buffers(4, half),
                dma((3,)), dma((2,)), dma((2,)),
                dma((n,)), dma((n,)), dma((n,)), dma((n,)),
                *semaphores(2),
                *semaphores(4),
            ],
            compiler_params=pltpu.CompilerParams(
                collective_id=0, has_side_effects=True, vmem_limit_bytes=24 * 1024 * 1024
            ),
        )(dosage, trait_class.reshape(1, depth), class_effect)

    in_specs = (P("smp", "var"), P("smp"), P())
    out_specs = P(("var", "smp"), None)
    return jax.shard_map(shards, mesh=mesh, in_specs=in_specs, out_specs=out_specs, check_vma=False)
```

```python
import functools

import jax
import jax.numpy as jnp
from jax import lax
from jax.experimental import pallas as pl
from jax.experimental.pallas import tpu as pltpu
from jax.sharding import PartitionSpec as P

MESH = pl.DeviceIdType.MESH
F32, BF16 = jnp.float32, jnp.bfloat16
LANES = 128


def kernel(
    nv, n, dosage_ref, class_hbm, effect_hbm, out_ref,
    d_ref, class_ref, effect_ref, after, wt, qt, sq, turned, before, own_turned, mirrored,
    own_part, own_wire, own_relay, own_fwd, own_summed, own_direct,
    next_part, next_wire, next_relay, next_fwd, next_summed, next_direct,
    load_sem, d_send, d_recv, t_send, t_recv, m_send, m_recv,
    own_rs, own_rr, own_fs, own_sr, own_ds, own_dr,
    next_rs, next_rr, next_fs, next_sr, next_ds, next_dr,
):
    depth, width = d_ref.shape
    rows, half, pairs = width // n, width // 2, n // 2
    fold = rows % LANES == 0
    v, s = lax.axis_index("var"), lax.axis_index("smp")
    nxt, prv = lax.rem(v + 1, nv), lax.rem(v + nv - 1, nv)
    pair, odd = s // 2, lax.rem(s, 2)
    partner = s + 1 - 2 * odd

    loads = [
        pltpu.make_async_copy(dosage_ref, d_ref, load_sem.at[0]),
        pltpu.make_async_copy(class_hbm, class_ref, load_sem.at[1]),
        pltpu.make_async_copy(effect_hbm, effect_ref, load_sem.at[2]),
    ]
    for load in loads:
        load.start()
    barrier = pltpu.get_barrier_semaphore()
    for near in (nxt, prv):
        for step in range(n):
            pl.semaphore_signal(barrier, inc=1, device_id=(near, lax.rem(s + step, n)), device_id_type=MESH)
    for step in range(1, n):
        pl.semaphore_signal(barrier, inc=1, device_id=(v, lax.rem(s + step, n)), device_id_type=MESH)
    for load in loads:
        load.wait()

    def cols(h):
        return slice(h * half, (h + 1) * half)

    def shift(h):
        return pltpu.make_async_remote_copy(
            src_ref=d_ref.at[:, cols(h)], dst_ref=after.at[:, cols(h)],
            send_sem=d_send.at[h], recv_sem=d_recv.at[h],
            device_id=(prv, s), device_id_type=MESH,
        )

    classes = effect_ref.shape[0]
    mean = effect_ref[0]
    for c in range(1, classes):
        mean = mean + effect_ref[c]
    mean = mean / classes
    picked = class_ref[...]
    trait = jnp.zeros(picked.shape, F32)
    for c in range(classes):
        trait = jnp.where(picked == c, effect_ref[c] - mean, trait)
    for at in range(0, width, LANES):
        values = d_ref[:, at:at + LANES].astype(F32).T
        wt[at:at + LANES, :] = (values * trait).astype(BF16)
        qt[at:at + LANES, :] = (values * values).astype(BF16)

    def owns(a, c):
        from_a, from_c = abs_of(2 * a - (n - 1)), abs_of(2 * c - (n - 1))
        return jnp.logical_or(from_a > from_c, jnp.logical_and(from_a == from_c, a < c))

    def abs_of(x):
        return lax.max(x, -x) if isinstance(x, jax.Array) else jnp.int32(abs(x))

    def extent(t):
        if not fold:
            return slice(0, width)
        first, last = (t, n - 1 - t) if t < pairs else (n - t, t)
        return slice(first * rows, (last + 1) * rows)

    def cases(index, count, body):
        for known in range(count):
            pl.when(index == known)(functools.partial(body, known))

    def at_rows(index):
        return pl.ds(pl.multiple_of(index * rows, rows), rows)

    def outer(k):
        higher = lax.rem(pair + k, pairs) > pair
        return jnp.logical_or(
            jnp.logical_and(higher, odd == 0), jnp.logical_and(jnp.logical_not(higher), odd == 1)
        )

    class Group:
        def __init__(self, folded, part, wire, relay, fwd, summed, direct, rs, rr, fs, sr, ds, dr):
            self.folded, self.part, self.wire, self.relay = folded, part, wire, relay
            self.fwd, self.summed, self.direct = fwd, summed, direct
            self.rs, self.rr, self.fs, self.sr, self.ds, self.dr = rs, rr, fs, sr, ds, dr

        def span(self, t):
            return extent(t) if self.folded else slice(None)

        def by(self, index, count, body):
            if self.folded:
                cases(index, count, body)
            else:
                body(index)

        def relay_copy(self, u, other, j):
            t = 2 * other + j
            span = self.span(t)
            return pltpu.make_async_remote_copy(
                src_ref=self.wire.at[u, at_rows(t), span], dst_ref=self.relay.at[u, other, j, :, span],
                send_sem=self.rs.at[u, other, j], recv_sem=self.rr.at[u, other, j],
                device_id=(v, partner), device_id_type=MESH,
            )

        def fwd_copy(self, u, other, j):
            t = 2 * other + j
            span = self.span(t)
            return pltpu.make_async_remote_copy(
                src_ref=self.fwd.at[u, other, j, :, span], dst_ref=self.summed.at[u, pair, :, span],
                send_sem=self.fs.at[u, other, j], recv_sem=self.sr.at[u, pair],
                device_id=(v, t), device_id_type=MESH,
            )

        def sum_wait(self, u, source, t):
            span = self.span(t)
            here = self.summed.at[u, source, :, span]
            pltpu.make_async_remote_copy(
                src_ref=here, dst_ref=here, send_sem=self.fs.at[u, source, 0], recv_sem=self.sr.at[u, source],
                device_id=(v, partner), device_id_type=MESH,
            ).wait_recv()

        def dir_copy(self, u, t):
            span = self.span(t)
            return pltpu.make_async_remote_copy(
                src_ref=self.wire.at[u, at_rows(t), span], dst_ref=self.direct.at[u, :, span],
                send_sem=self.ds.at[u], recv_sem=self.dr.at[u],
                device_id=(v, partner), device_id_type=MESH,
            )

        def product(self, u, left, right):
            got = jnp.dot(left[...], right, preferred_element_type=F32)
            self.part[u] = got
            self.wire[u] = got.astype(BF16)

        def send_relays(self, u):
            for k in range(1, pairs):
                @pl.when(outer(k))
                def _():
                    def send(other):
                        for j in range(2):
                            self.relay_copy(u, other, j).start()

                    self.by(lax.rem(pair + k, pairs), pairs, send)

        def send_sums(self, u):
            for k in range(1, pairs):
                @pl.when(jnp.logical_not(outer(k)))
                def _():
                    def send(other):
                        for j in range(2):
                            self.relay_copy(u, other, j).wait_recv()
                            own = self.part[u, at_rows(2 * other + j), :]
                            self.fwd[u, other, j] = (own + self.relay[u, other, j].astype(F32)).astype(BF16)
                            self.fwd_copy(u, other, j).start()

                    self.by(lax.rem(pair + k, pairs), pairs, send)

        def send_direct(self, u):
            self.by(partner, n, lambda t: self.dir_copy(u, t).start())

        def total(self, u):
            def wait(t):
                self.dir_copy(u, t).wait_recv()
                for k in range(1, pairs):
                    self.sum_wait(u, lax.rem(pair + k, pairs), t)

            self.by(s, n, wait)
            got = self.part[u, at_rows(s), :] + self.direct[u].astype(F32)
            for k in range(1, pairs):
                got = got + self.summed[u, lax.rem(pair + k, pairs)].astype(F32)
            return got

        def finish(self, units):
            for u in range(units):
                self.by(partner, n, lambda t: self.dir_copy(u, t).wait_send())
                for k in range(1, pairs):
                    def relays(other):
                        for j in range(2):
                            self.relay_copy(u, other, j).wait_send()

                    def sums(other):
                        for j in range(2):
                            self.fwd_copy(u, other, j).wait_send()

                    other = lax.rem(pair + k, pairs)

                    @pl.when(outer(k))
                    def _():
                        self.by(other, pairs, relays)

                    @pl.when(jnp.logical_not(outer(k)))
                    def _():
                        self.by(other, pairs, sums)

    own = Group(
        fold, own_part, own_wire, own_relay, own_fwd, own_summed, own_direct,
        own_rs, own_rr, own_fs, own_sr, own_ds, own_dr,
    )
    follow = Group(
        False, next_part, next_wire, next_relay, next_fwd, next_summed, next_direct,
        next_rs, next_rr, next_fs, next_sr, next_ds, next_dr,
    )

    def squares(values):
        values = values.astype(F32)
        return (values * values).astype(BF16)

    own.product(0, wt, d_ref[...])
    pl.semaphore_wait(barrier, 3 * n - 1)
    for h in range(2):
        shift(h).start()
    own.send_relays(0)
    sq[...] = squares(d_ref[...])
    own.product(1, qt, sq[...])
    own.send_relays(1)
    late = outer(1) if pairs > 1 else jnp.logical_and(odd == 0, odd == 1)

    @pl.when(jnp.logical_not(late))
    def _():
        for u in range(2):
            own.send_direct(u)

    for h in range(2):
        shift(h).wait_recv()
        follow.product(2 * h, wt, after[:, cols(h)])
        follow.send_relays(2 * h)
        sq[:, cols(h)] = squares(after[:, cols(h)])
        follow.product(2 * h + 1, qt, sq[:, cols(h)])
        follow.send_relays(2 * h + 1)

        @pl.when(jnp.logical_not(late))
        def _():
            for u in range(2 * h, 2 * h + 2):
                follow.send_direct(u)

        if h == 0:
            for u in range(2):
                own.send_sums(u)

    @pl.when(late)
    def _():
        for u in range(4):
            follow.send_direct(u)
        for u in range(2):
            own.send_direct(u)

    for u in range(4):
        follow.send_sums(u)

    def turn_copy(t, slot):
        return pltpu.make_async_remote_copy(
            src_ref=turned.at[t * rows:(t + 1) * rows], dst_ref=before.at[slot],
            send_sem=t_send.at[t], recv_sem=t_recv.at[slot],
            device_id=(nxt, t), device_id_type=MESH,
        )

    def mirror_copy(t, slot):
        return pltpu.make_async_remote_copy(
            src_ref=own_turned.at[t * rows:(t + 1) * rows], dst_ref=mirrored.at[slot],
            send_sem=m_send.at[t], recv_sem=m_recv.at[slot],
            device_id=(v, t), device_id_type=MESH,
        )

    for h in range(2):
        stat = follow.total(2 * h) / jnp.sqrt(follow.total(2 * h + 1) + 1e-05)
        out_ref[:, 2 * width + h * half:2 * width + (h + 1) * half] = stat
        turned[cols(h), :] = stat.T.astype(BF16)
        for t in range(h * pairs, (h + 1) * pairs):
            turn_copy(t, s).start()
    stat = own.total(0) / jnp.sqrt(own.total(1) + 1e-05)
    if fold:
        own_turned[...] = stat.T.astype(BF16)
        for t in range(n):
            @pl.when(owns(s, t))
            def _():
                mirror_copy(t, s).start()
    out_ref[:, width:2 * width] = stat
    for t in range(n):
        turn_copy(t, t).wait_recv()
        out_ref[:, t * rows:(t + 1) * rows] = before[t].astype(F32)
    if fold:
        for t in range(n):
            @pl.when(owns(t, s))
            def _():
                mirror_copy(t, t).wait_recv()
                out_ref[:, width + t * rows:width + (t + 1) * rows] = mirrored[t].astype(F32)

            @pl.when(owns(s, t))
            def _():
                mirror_copy(t, t).wait_send()

    for h in range(2):
        shift(h).wait_send()
    own.finish(2)
    follow.finish(4)
    for t in range(n):
        turn_copy(t, t).wait_send()


def solution(mesh):
    nv, n = mesh.shape["var"], mesh.shape["smp"]

    def shards(dosage, trait_class, class_effect):
        depth, width = dosage.shape
        rows, half, pairs = width // n, width // 2, n // 2
        dma, vmem = pltpu.SemaphoreType.DMA, pltpu.VMEM

        def buffers(units, wide):
            return [
                vmem((units, width, wide), F32),
                vmem((units, width, wide), BF16),
                vmem((units, pairs, 2, rows, wide), BF16),
                vmem((units, pairs, 2, rows, wide), BF16),
                vmem((units, pairs, rows, wide), BF16),
                vmem((units, rows, wide), BF16),
            ]

        def semaphores(units):
            return [
                dma((units, pairs, 2)), dma((units, pairs, 2)), dma((units, pairs, 2)),
                dma((units, pairs)), dma((units,)), dma((units,)),
            ]

        return pl.pallas_call(
            functools.partial(kernel, nv, n),
            out_shape=jax.ShapeDtypeStruct((rows, 3 * width), F32),
            in_specs=[pl.BlockSpec(memory_space=pltpu.HBM)] * 3,
            out_specs=pl.BlockSpec(memory_space=vmem),
            scratch_shapes=[
                vmem((depth, width), BF16),
                vmem((1, depth), jnp.int32),
                pltpu.SMEM(class_effect.shape, F32),
                vmem((depth, width), BF16),
                vmem((width, depth), BF16),
                vmem((width, depth), BF16),
                vmem((depth, width), BF16),
                vmem((width, rows), BF16),
                vmem((n, rows, rows), BF16),
                vmem((width, rows), BF16),
                vmem((n, rows, rows), BF16),
                *buffers(2, width),
                *buffers(4, half),
                dma((3,)), dma((2,)), dma((2,)),
                dma((n,)), dma((n,)), dma((n,)), dma((n,)),
                *semaphores(2),
                *semaphores(4),
            ],
            compiler_params=pltpu.CompilerParams(
                collective_id=0, has_side_effects=True, vmem_limit_bytes=24 * 1024 * 1024
            ),
        )(*(pltpu.with_memory_space_constraint(x, pltpu.HBM) for x in (dosage, trait_class.reshape(1, depth), class_effect)))

    in_specs = (P("smp", "var"), P("smp"), P())
    out_specs = P(("var", "smp"), None)
    return jax.shard_map(shards, mesh=mesh, in_specs=in_specs, out_specs=out_specs, check_vma=False)
```

```python
import functools

import jax
import jax.numpy as jnp
from jax import lax
from jax.experimental import pallas as pl
from jax.experimental.pallas import tpu as pltpu
from jax.sharding import PartitionSpec as P

MESH = pl.DeviceIdType.MESH
F32, BF16 = jnp.float32, jnp.bfloat16
LANES = 128


def kernel(
    nv, n, dosage_ref, class_hbm, effect_hbm, out_ref,
    d_ref, class_ref, effect_ref, after, wt, qt, sq, turned, before, own_turned, mirrored,
    own_part, own_wire, own_relay, own_fwd, own_summed, own_direct,
    next_part, next_wire, next_relay, next_fwd, next_summed, next_direct,
    load_sem, d_send, d_recv, t_send, t_recv, m_send, m_recv,
    own_rs, own_rr, own_fs, own_sr, own_ds, own_dr,
    next_rs, next_rr, next_fs, next_sr, next_ds, next_dr,
):
    depth, width = d_ref.shape
    rows, half, pairs = width // n, width // 2, n // 2
    fold = rows % LANES == 0
    v, s = lax.axis_index("var"), lax.axis_index("smp")
    nxt, prv = lax.rem(v + 1, nv), lax.rem(v + nv - 1, nv)
    pair, odd = s // 2, lax.rem(s, 2)
    partner = s + 1 - 2 * odd

    loads = [
        pltpu.make_async_copy(dosage_ref, d_ref, load_sem.at[0]),
        pltpu.make_async_copy(class_hbm, class_ref, load_sem.at[1]),
        pltpu.make_async_copy(effect_hbm, effect_ref, load_sem.at[2]),
    ]
    for load in loads:
        load.start()
    barrier = pltpu.get_barrier_semaphore()
    for near in (nxt, prv):
        for step in range(n):
            pl.semaphore_signal(barrier, inc=1, device_id=(near, lax.rem(s + step, n)), device_id_type=MESH)
    for step in range(1, n):
        pl.semaphore_signal(barrier, inc=1, device_id=(v, lax.rem(s + step, n)), device_id_type=MESH)
    for load in loads:
        load.wait()

    def cols(h):
        return slice(h * half, (h + 1) * half)

    def shift(h):
        return pltpu.make_async_remote_copy(
            src_ref=d_ref.at[:, cols(h)], dst_ref=after.at[:, cols(h)],
            send_sem=d_send.at[h], recv_sem=d_recv.at[h],
            device_id=(prv, s), device_id_type=MESH,
        )

    classes = effect_ref.shape[0]
    mean = effect_ref[0]
    for c in range(1, classes):
        mean = mean + effect_ref[c]
    mean = mean / classes
    picked = class_ref[...]
    trait = jnp.zeros(picked.shape, F32)
    for c in range(classes):
        trait = jnp.where(picked == c, effect_ref[c] - mean, trait)
    for at in range(0, width, LANES):
        values = d_ref[:, at:at + LANES].astype(F32).T
        wt[at:at + LANES, :] = (values * trait).astype(BF16)
        qt[at:at + LANES, :] = (values * values).astype(BF16)

    def owns(a, c):
        from_a, from_c = abs_of(2 * a - (n - 1)), abs_of(2 * c - (n - 1))
        return jnp.logical_or(from_a > from_c, jnp.logical_and(from_a == from_c, a < c))

    def abs_of(x):
        return lax.max(x, -x) if isinstance(x, jax.Array) else jnp.int32(abs(x))

    def extent(t):
        if not fold:
            return slice(0, width)
        first, last = (t, n - 1 - t) if t < pairs else (n - t, t)
        return slice(first * rows, (last + 1) * rows)

    def cases(index, count, body):
        for known in range(count):
            pl.when(index == known)(functools.partial(body, known))

    def at_rows(index):
        return pl.ds(pl.multiple_of(index * rows, rows), rows)

    def outer(k):
        higher = lax.rem(pair + k, pairs) > pair
        return jnp.logical_or(
            jnp.logical_and(higher, odd == 0), jnp.logical_and(jnp.logical_not(higher), odd == 1)
        )

    class Group:
        def __init__(self, folded, part, wire, relay, fwd, summed, direct, rs, rr, fs, sr, ds, dr):
            self.folded, self.part, self.wire, self.relay = folded, part, wire, relay
            self.fwd, self.summed, self.direct = fwd, summed, direct
            self.rs, self.rr, self.fs, self.sr, self.ds, self.dr = rs, rr, fs, sr, ds, dr

        def span(self, t):
            return extent(t) if self.folded else slice(None)

        def by(self, index, count, body):
            if self.folded:
                cases(index, count, body)
            else:
                body(index)

        def relay_copy(self, u, other, j):
            t = 2 * other + j
            span = self.span(t)
            return pltpu.make_async_remote_copy(
                src_ref=self.wire.at[u, at_rows(t), span], dst_ref=self.relay.at[u, other, j, :, span],
                send_sem=self.rs.at[u, other, j], recv_sem=self.rr.at[u, other, j],
                device_id=(v, partner), device_id_type=MESH,
            )

        def fwd_copy(self, u, other, j):
            t = 2 * other + j
            span = self.span(t)
            return pltpu.make_async_remote_copy(
                src_ref=self.fwd.at[u, other, j, :, span], dst_ref=self.summed.at[u, pair, :, span],
                send_sem=self.fs.at[u, other, j], recv_sem=self.sr.at[u, pair],
                device_id=(v, t), device_id_type=MESH,
            )

        def sum_wait(self, u, source, t):
            span = self.span(t)
            here = self.summed.at[u, source, :, span]
            pltpu.make_async_remote_copy(
                src_ref=here, dst_ref=here, send_sem=self.fs.at[u, source, 0], recv_sem=self.sr.at[u, source],
                device_id=(v, partner), device_id_type=MESH,
            ).wait_recv()

        def dir_copy(self, u, t):
            span = self.span(t)
            return pltpu.make_async_remote_copy(
                src_ref=self.wire.at[u, at_rows(t), span], dst_ref=self.direct.at[u, :, span],
                send_sem=self.ds.at[u], recv_sem=self.dr.at[u],
                device_id=(v, partner), device_id_type=MESH,
            )

        def product(self, u, left, right):
            got = jnp.dot(left[...], right, preferred_element_type=F32)
            self.part[u] = got
            self.wire[u] = got.astype(BF16)

        def send_relays(self, u):
            for k in range(1, pairs):
                @pl.when(outer(k))
                def _():
                    def send(other):
                        for j in range(2):
                            self.relay_copy(u, other, j).start()

                    self.by(lax.rem(pair + k, pairs), pairs, send)

        def send_sums(self, u):
            for k in range(1, pairs):
                @pl.when(jnp.logical_not(outer(k)))
                def _():
                    def send(other):
                        for j in range(2):
                            self.relay_copy(u, other, j).wait_recv()
                            own = self.part[u, at_rows(2 * other + j), :]
                            self.fwd[u, other, j] = (own + self.relay[u, other, j].astype(F32)).astype(BF16)
                            self.fwd_copy(u, other, j).start()

                    self.by(lax.rem(pair + k, pairs), pairs, send)

        def send_direct(self, u):
            self.by(partner, n, lambda t: self.dir_copy(u, t).start())

        def total(self, u):
            def wait(t):
                self.dir_copy(u, t).wait_recv()
                for k in range(1, pairs):
                    self.sum_wait(u, lax.rem(pair + k, pairs), t)

            self.by(s, n, wait)
            got = self.part[u, at_rows(s), :] + self.direct[u].astype(F32)
            for k in range(1, pairs):
                got = got + self.summed[u, lax.rem(pair + k, pairs)].astype(F32)
            return got

        def finish(self, units):
            for u in range(units):
                self.by(partner, n, lambda t: self.dir_copy(u, t).wait_send())
                for k in range(1, pairs):
                    def relays(other):
                        for j in range(2):
                            self.relay_copy(u, other, j).wait_send()

                    def sums(other):
                        for j in range(2):
                            self.fwd_copy(u, other, j).wait_send()

                    other = lax.rem(pair + k, pairs)

                    @pl.when(outer(k))
                    def _():
                        self.by(other, pairs, relays)

                    @pl.when(jnp.logical_not(outer(k)))
                    def _():
                        self.by(other, pairs, sums)

    own = Group(
        fold, own_part, own_wire, own_relay, own_fwd, own_summed, own_direct,
        own_rs, own_rr, own_fs, own_sr, own_ds, own_dr,
    )
    follow = Group(
        False, next_part, next_wire, next_relay, next_fwd, next_summed, next_direct,
        next_rs, next_rr, next_fs, next_sr, next_ds, next_dr,
    )

    def squares(values):
        values = values.astype(F32)
        return (values * values).astype(BF16)

    own.product(0, wt, d_ref[...])
    pl.semaphore_wait(barrier, 3 * n - 1)
    for h in range(2):
        shift(h).start()
    own.send_relays(0)
    sq[...] = squares(d_ref[...])
    own.product(1, qt, sq[...])
    own.send_relays(1)
    late = outer(1) if pairs > 1 else jnp.logical_and(odd == 0, odd == 1)

    for u in range(2):
        own.send_direct(u)
    for h in range(2):
        shift(h).wait_recv()
        follow.product(2 * h, wt, after[:, cols(h)])
        follow.send_relays(2 * h)
        sq[:, cols(h)] = squares(after[:, cols(h)])
        follow.product(2 * h + 1, qt, sq[:, cols(h)])
        follow.send_relays(2 * h + 1)

        @pl.when(jnp.logical_not(late))
        def _():
            for u in range(2 * h, 2 * h + 2):
                follow.send_direct(u)

        if h == 0:
            for u in range(2):
                own.send_sums(u)

    @pl.when(late)
    def _():
        for u in range(4):
            follow.send_direct(u)

    for u in range(4):
        follow.send_sums(u)

    def turn_copy(t, slot):
        return pltpu.make_async_remote_copy(
            src_ref=turned.at[t * rows:(t + 1) * rows], dst_ref=before.at[slot],
            send_sem=t_send.at[t], recv_sem=t_recv.at[slot],
            device_id=(nxt, t), device_id_type=MESH,
        )

    def mirror_copy(t, slot):
        return pltpu.make_async_remote_copy(
            src_ref=own_turned.at[t * rows:(t + 1) * rows], dst_ref=mirrored.at[slot],
            send_sem=m_send.at[t], recv_sem=m_recv.at[slot],
            device_id=(v, t), device_id_type=MESH,
        )

    for h in range(2):
        stat = follow.total(2 * h) / jnp.sqrt(follow.total(2 * h + 1) + 1e-05)
        out_ref[:, 2 * width + h * half:2 * width + (h + 1) * half] = stat
        turned[cols(h), :] = stat.T.astype(BF16)
        for t in range(h * pairs, (h + 1) * pairs):
            turn_copy(t, s).start()
    stat = own.total(0) / jnp.sqrt(own.total(1) + 1e-05)
    if fold:
        own_turned[...] = stat.T.astype(BF16)
        for t in range(n):
            @pl.when(owns(s, t))
            def _():
                mirror_copy(t, s).start()
    out_ref[:, width:2 * width] = stat
    for t in range(n):
        turn_copy(t, t).wait_recv()
        out_ref[:, t * rows:(t + 1) * rows] = before[t].astype(F32)
    if fold:
        for t in range(n):
            @pl.when(owns(t, s))
            def _():
                mirror_copy(t, t).wait_recv()
                out_ref[:, width + t * rows:width + (t + 1) * rows] = mirrored[t].astype(F32)

            @pl.when(owns(s, t))
            def _():
                mirror_copy(t, t).wait_send()

    for h in range(2):
        shift(h).wait_send()
    own.finish(2)
    follow.finish(4)
    for t in range(n):
        turn_copy(t, t).wait_send()


def solution(mesh):
    nv, n = mesh.shape["var"], mesh.shape["smp"]

    def shards(dosage, trait_class, class_effect):
        depth, width = dosage.shape
        rows, half, pairs = width // n, width // 2, n // 2
        dma, vmem = pltpu.SemaphoreType.DMA, pltpu.VMEM

        def buffers(units, wide):
            return [
                vmem((units, width, wide), F32),
                vmem((units, width, wide), BF16),
                vmem((units, pairs, 2, rows, wide), BF16),
                vmem((units, pairs, 2, rows, wide), BF16),
                vmem((units, pairs, rows, wide), BF16),
                vmem((units, rows, wide), BF16),
            ]

        def semaphores(units):
            return [
                dma((units, pairs, 2)), dma((units, pairs, 2)), dma((units, pairs, 2)),
                dma((units, pairs)), dma((units,)), dma((units,)),
            ]

        return pl.pallas_call(
            functools.partial(kernel, nv, n),
            out_shape=jax.ShapeDtypeStruct((rows, 3 * width), F32),
            in_specs=[pl.BlockSpec(memory_space=pltpu.HBM)] * 3,
            out_specs=pl.BlockSpec(memory_space=vmem),
            scratch_shapes=[
                vmem((depth, width), BF16),
                vmem((1, depth), jnp.int32),
                pltpu.SMEM(class_effect.shape, F32),
                vmem((depth, width), BF16),
                vmem((width, depth), BF16),
                vmem((width, depth), BF16),
                vmem((depth, width), BF16),
                vmem((width, rows), BF16),
                vmem((n, rows, rows), BF16),
                vmem((width, rows), BF16),
                vmem((n, rows, rows), BF16),
                *buffers(2, width),
                *buffers(4, half),
                dma((3,)), dma((2,)), dma((2,)),
                dma((n,)), dma((n,)), dma((n,)), dma((n,)),
                *semaphores(2),
                *semaphores(4),
            ],
            compiler_params=pltpu.CompilerParams(
                collective_id=0, has_side_effects=True, vmem_limit_bytes=24 * 1024 * 1024
            ),
        )(*(pltpu.with_memory_space_constraint(x, pltpu.HBM) for x in (dosage, trait_class.reshape(1, depth), class_effect)))

    in_specs = (P("smp", "var"), P("smp"), P())
    out_specs = P(("var", "smp"), None)
    return jax.shard_map(shards, mesh=mesh, in_specs=in_specs, out_specs=out_specs, check_vma=False)
```
